512 devices in a mesh: req: 32 (over z, y_lo), tp: 16 (over y_hi, x, core).
Axes of the slice: x: 4, y: 8 (y_hi: 2, y_lo: 4; y = y_hi * 4 + y_lo), z: 8, core: 2. Of those that a mesh axis runs over, the one named last changes fastest.
Arguments:
- tokens: bfloat16 [16384, 4096], P(('req', 'tp')), parts along dimension 0, may hold values from -400 to 400
- norm_gain: bfloat16 [4096], replicated, may hold values from 0.099609375 to 1.8984375
- qkv_weight: bfloat16 [4096, 6144], P(None, 'tp'), may hold values from -0.46875 to 0.46875
- out_weight: bfloat16 [2048, 4096], P('tp'), may hold values from -0.5 to 0.5
- segment_ids: int32 [16384], P('req'), parts along dimension 0, may hold values from 0 to 7, never falling along the last dimension, each value on 1 to 170 neighbouring positions
- prefix_pages: int32 [256], P('req'), parts along dimension 0, may hold values from 1 to 16, 48 in all
- page_order: int32 [1536], P('req'), parts along dimension 0, may hold values from 0 to 47, each once
- fresh_order: int32 [1280], P('req'), parts along dimension 0, may hold values from 0 to 39, each once
- cache_pool: bfloat16 [2, 16, 1536, 16, 128], P(None, 'tp', 'req'), parts along dimension 2, may hold values from -6 to 6
Outputs:
- attn_out: bfloat16 [16384, 4096], P(('req', 'tp')), parts along dimension 0
- fresh_pages: bfloat16 [2, 16, 1280, 16, 128], P(None, 'tp', 'req'), parts along dimension 2
The draws below stay inside these ranges and needn't reach their ends.
There are 32 independent parts, one for each index of `req`. The reference program is written for one: setup_inputs(seed, part) draws one part's arguments, and reference() takes and returns one part's arrays. A program takes and returns all parts, laid end to end along the dimension named above; an argument that names none is the same for every part. Nothing has to cross between parts.
Inputs may be any that keep to these rules, and one draw needn't show every extreme that they name: `segment_ids`: segment numbers never fall; every prompt has at least one new token and one has exactly 170. `prefix_pages`: they sum to 48; the largest is 16. `page_order`: every page once. `fresh_order`: every page once.
All inputs are finite; a program needn't handle non-finite values.
Results may differ from the reference program's by a relative error of at most 0.014.
Values may be sent and summed in bfloat16 or wider, within the bound.
No kernel may reach another device: no remote copies, remote signals or barrier semaphores. Data moves between devices by JAX's collectives and lax.ppermute only.
A program may use at most 64 MiB of HBM per device.

```python
import math
import jax
import jax.numpy as jnp
import numpy as np
from jax import lax

D = 4096
HEAD_SIZE = 128
MODEL_HEADS = 32
HEAD_DEV = 1
SEQS = 8
PAGE_LEN = 16
CACHE_PAGES = 48
HEADS = 16
TOKENS = 512
MAXP = 16
SEG_MOST = 170
FRESH_PAGES = 40
N_TP = 16


def draw_tokens(key, part):
    keys_all = jax.random.split(key, 3)
    row_scale = jnp.exp(jax.random.uniform(keys_all[0], (TOKENS // 2, 1), jnp.float32) * jnp.log(10.0))
    row_scale = jnp.repeat(row_scale, 2, axis=0)
    col_scale = jnp.exp(jax.random.uniform(keys_all[1], (1, D), jnp.float32) * jnp.log(10.0))
    paired = jax.random.normal(keys_all[2], (TOKENS, D), jnp.float32)
    return (jnp.clip(paired, -4.0, 4.0) * row_scale * col_scale).astype(jnp.bfloat16)


def draw_qkv_weight(key, part):
    keys_all = jax.random.split(key, 1)
    stacked = jnp.clip(jax.random.normal(keys_all[0], (D, HEADS, 3, HEAD_SIZE), jnp.float32), -5.0, 5.0)
    return (stacked * D ** (-0.5)).reshape(D, HEADS * 3 * HEAD_SIZE).astype(jnp.bfloat16)


def levels(key, shape, shards, low, largest):
    level = 1.0
    for dim, blocks in shards:
        heights = jax.random.uniform(jax.random.fold_in(jax.random.fold_in(key, 6), dim), (blocks,), jnp.float32, low / len(shards), largest / len(shards))
        level = level * jnp.repeat(jnp.exp(heights), shape[dim] // blocks).reshape((-1,) + (1,) * (len(shape) - 1 - dim))
    return level


def split_up(amount, total, most, slope):
    portions = [(1 << 20) // math.isqrt(grade ** slope) + 1 for grade in range(2, amount + 1)]
    surplus, holding = total - most - (amount - 1), [1] * (amount - 1)
    while surplus > 0:
        free = [i for i in range(amount - 1) if holding[i] < most]
        whole, left = sum([portions[i] for i in free]), surplus
        for i in free:
            extra = min(most - holding[i], max(1, left * portions[i] // whole), surplus)
            holding[i] = holding[i] + extra
            surplus = surplus - extra
    return np.array([most] + holding)


def uneven(key, amount, total, reach, lean):
    if amount == 2:
        one = jax.random.randint(key, (), max(1, total - reach), min(reach, total - 1) + 1)
        return jnp.stack([one, total - one])
    lengths = jnp.asarray(split_up(amount, total, reach, lean), jnp.int32)
    pairs = (amount - 1) // 2
    giver, taker = lengths[1:1 + 2 * pairs:2], lengths[2:2 + 2 * pairs:2]
    room = jnp.minimum(giver - 1, reach - taker)
    moved = jax.random.randint(jax.random.fold_in(key, 1), (pairs,), 0, 1 << 20) % (room + 1)
    lengths = lengths.at[1:1 + 2 * pairs:2].set(giver - moved).at[2:2 + 2 * pairs:2].set(taker + moved)
    return lengths[jax.random.permutation(jax.random.fold_in(key, 2), amount)]


def bell_draw(key, extent, scale, limit, shards=(), held_as=jnp.bfloat16):
    level = levels(key, extent, shards, -0.22, 0.18) if shards else 1.0
    result = jax.random.normal(key, extent, jnp.float32) * scale * level
    return jnp.minimum(jnp.maximum(result, -limit), limit).astype(held_as)


def setup_inputs(seed: int = 0, part: int = 0) -> dict:
    key_list = jax.random.split(jax.random.key(seed), 10)
    part_keys = jax.random.split(jax.random.fold_in(key_list[9], part), 10)
    tokens = draw_tokens(jax.random.fold_in(jax.random.fold_in(key_list[9], part), 71), part)
    norm_gain = jnp.clip(1.0 + 0.18 * jax.random.normal(key_list[1], (D,), jnp.float32), 0.099609375, 1.8984375).astype(jnp.bfloat16)
    qkv_weight = draw_qkv_weight(jax.random.fold_in(key_list[9], 71), part)
    out_weight = bell_draw(key_list[3], (HEADS * HEAD_SIZE, D), HEAD_SIZE ** -0.5, 0.5, ((0, 16),))
    segment_ids = jnp.searchsorted(jnp.cumsum(uneven(part_keys[4], SEQS, TOKENS, SEG_MOST, 2)), jnp.arange(TOKENS), side="right").astype(jnp.int32)
    prefix_pages = uneven(part_keys[5], SEQS, CACHE_PAGES, MAXP, 2).astype(jnp.int32)
    page_order = jax.random.permutation(part_keys[6], CACHE_PAGES).astype(jnp.int32)
    fresh_order = jax.random.permutation(part_keys[7], FRESH_PAGES).astype(jnp.int32)
    cache_pool = bell_draw(part_keys[8], (2, HEADS, CACHE_PAGES, PAGE_LEN, HEAD_SIZE), 1.0, 6.0, ((1, 16),))
    return dict(tokens=tokens, norm_gain=norm_gain, qkv_weight=qkv_weight, out_weight=out_weight, segment_ids=segment_ids, prefix_pages=prefix_pages, page_order=page_order, fresh_order=fresh_order, cache_pool=cache_pool)


def layer_norm(values, gain):
    values = values.astype(jnp.float32)
    center = values - lax.optimization_barrier(jnp.mean(values, axis=-1, keepdims=True))
    spread = lax.optimization_barrier(jnp.mean(center * center, axis=-1, keepdims=True))
    return (center * lax.rsqrt(spread + 1e-05) * gain.astype(jnp.float32)).astype(jnp.bfloat16)

def token_layout(segment_ids, prefix_pages, page_order, fresh_order, page_len):
    seq_count = prefix_pages.shape[0]
    tok_count = segment_ids.shape[0]
    labels = jnp.arange(seq_count, dtype=jnp.int32)
    member = (segment_ids[:, None] == labels[None, :]).astype(jnp.int32)
    counts = lax.optimization_barrier(jnp.sum(member, axis=0)).astype(jnp.int32)
    starts = (jnp.cumsum(counts) - counts).astype(jnp.int32)
    token_index = jnp.arange(tok_count, dtype=jnp.int32)
    in_prompt = (token_index - lax.optimization_barrier(jnp.sum(member * starts[None, :], axis=1))).astype(jnp.int32)
    prefix_len = prefix_pages * page_len
    position = (in_prompt + lax.optimization_barrier(jnp.sum(member * prefix_len[None, :], axis=1))).astype(jnp.int32)
    fresh_counts = (counts + page_len - 1) // page_len
    fresh_starts = (jnp.cumsum(fresh_counts) - fresh_counts).astype(jnp.int32)
    page_slot = (lax.optimization_barrier(jnp.sum(member * fresh_starts[None, :], axis=1)) + in_prompt // page_len).astype(jnp.int32)
    target = (jnp.take(fresh_order, page_slot) * page_len + in_prompt % page_len).astype(jnp.int32)
    page_count = page_order.shape[0]
    cache_starts = (jnp.cumsum(prefix_pages) - prefix_pages).astype(jnp.int32)
    logical = jnp.zeros((page_count,), jnp.int32).at[page_order].set(jnp.arange(page_count, dtype=jnp.int32))
    holder = (lax.optimization_barrier(jnp.sum((logical[:, None] >= cache_starts[None, :]).astype(jnp.int32), axis=1)) - 1).astype(jnp.int32)
    holder_start = lax.optimization_barrier(jnp.sum((holder[:, None] == labels[None, :]).astype(jnp.int32) * cache_starts[None, :], axis=1)).astype(jnp.int32)
    slot_index = jnp.arange(page_len, dtype=jnp.int32)
    key_owner = jnp.repeat(holder, page_len)
    key_pos = ((logical - holder_start)[:, None] * page_len + slot_index[None, :]).reshape(-1).astype(jnp.int32)
    return (in_prompt, position, target, key_owner, key_pos)

def attention_mask(segment_ids, in_prompt, position, key_owner, key_pos):
    cache_ok = segment_ids[:, None] == key_owner[None, :]
    new_ok = (segment_ids[:, None] == segment_ids[None, :]) & (in_prompt[None, :] <= in_prompt[:, None])
    allowed = jnp.concatenate([cache_ok, new_ok], axis=1)
    key_all = jnp.concatenate([key_pos, position])
    distance = (position[:, None] - key_all[None, :]).astype(jnp.float32)
    return (allowed, distance)

def attend_head(queries, key_rows, values, alibi_slope, allowed, distance):
    scores = lax.dot_general(queries, key_rows, (((1,), (1,)), ((), ())), preferred_element_type=jnp.float32)
    scores = scores * queries.shape[1] ** (-0.5) - alibi_slope * distance
    scores = jnp.where(allowed, scores, -1e+30)
    peak_score = lax.optimization_barrier(jnp.max(scores, axis=1, keepdims=True))
    weights = jnp.exp(scores - peak_score)
    weights_bf = (weights / lax.optimization_barrier(jnp.sum(weights, axis=1, keepdims=True))).astype(jnp.bfloat16)
    return jnp.dot(weights_bf, values, preferred_element_type=jnp.float32).astype(jnp.bfloat16)

def reference(tokens, norm_gain, qkv_weight, out_weight, segment_ids, prefix_pages, page_order, fresh_order, cache_pool):
    normed = layer_norm(tokens, norm_gain)
    projected = jnp.dot(normed, qkv_weight, preferred_element_type=jnp.float32).astype(jnp.bfloat16)
    in_prompt, position, target, key_owner, key_pos = token_layout(segment_ids, prefix_pages, page_order, fresh_order, PAGE_LEN)
    allowed, distance = attention_mask(segment_ids, in_prompt, position, key_owner, key_pos)
    per_head = projected.reshape(TOKENS, HEADS, 3, HEAD_SIZE).transpose(1, 2, 0, 3)
    step_heads = MODEL_HEADS // HEADS
    slopes = jnp.exp2(-8.0 * (jnp.arange(HEADS, dtype=jnp.float32) + 1.0) * step_heads / MODEL_HEADS)
    cache_flat = cache_pool.reshape(2, HEADS, CACHE_PAGES * PAGE_LEN, HEAD_SIZE).transpose(1, 0, 2, 3)

    def one_head(inputs):
        head_block, cached, alibi_slope = inputs
        key_rows = jnp.concatenate([cached[0], head_block[1]], axis=0)
        values = jnp.concatenate([cached[1], head_block[2]], axis=0)
        return attend_head(head_block[0], key_rows, values, alibi_slope, allowed, distance)
    context = lax.map(one_head, (per_head, cache_flat, slopes))
    groups = context.reshape(N_TP, HEAD_DEV, TOKENS, HEAD_SIZE).transpose(0, 2, 1, 3).reshape(N_TP, TOKENS, HEAD_DEV * HEAD_SIZE)
    weight_groups = out_weight.reshape(N_TP, HEAD_DEV * HEAD_SIZE, D)

    def add_group(running, inputs):
        group_ctx, weight = inputs
        rounded = jnp.dot(group_ctx, weight, preferred_element_type=jnp.float32).astype(jnp.bfloat16)
        rounded = lax.optimization_barrier(rounded)
        return (running + rounded.astype(jnp.float32), None)
    running, unused = lax.scan(add_group, jnp.zeros((TOKENS, D), jnp.float32), (groups, weight_groups))
    attn_out = running.astype(jnp.bfloat16)
    new_kv = per_head[:, 1:3].transpose(1, 0, 2, 3)
    fresh_pages = jnp.zeros((2, HEADS, FRESH_PAGES * PAGE_LEN, HEAD_SIZE), jnp.bfloat16).at[:, :, target].set(new_kv)
    return (attn_out, fresh_pages.reshape(2, HEADS, FRESH_PAGES, PAGE_LEN, HEAD_SIZE))
```

```python
import jax
import jax.numpy as jnp
from jax import lax
from jax.experimental import pallas as pl
from jax.experimental.pallas import tpu as pltpu
from jax.sharding import PartitionSpec as P


MODEL_HEADS = 32
N_X = 4
N_TP = 16
BLOCK = 32
PAGE = 16
SEQS = 8
HEAD = 128
FAR = 3e32


def tp_of(y, x, c):
    return (y % 2) * 8 + (x % N_X) * 2 + c % 2


def moved(value, dy, dx, dc):
    pairs = [
        (tp_of(y, x, c), tp_of(y + dy, x + dx, c + dc))
        for y in range(2)
        for x in range(N_X)
        for c in range(2)
    ]
    return lax.ppermute(value, "tp", pairs)


def my_place():
    me = lax.axis_index("tp")
    return me >> 3, (me >> 1) & 3, me & 1


def layout_kernel(seg_ref, prefix_ref, order_ref, fresh_ref, dist_ref, target_ref):
    y, x, c = my_place()
    seg = seg_ref[...]
    starts = [jnp.int32(0)]
    for s in range(1, SEQS):
        starts.append(jnp.sum((seg < s).astype(jnp.float32)).astype(jnp.int32))
    ends = starts[1:] + [jnp.int32(seg.shape[0] * seg.shape[1])]
    cache_starts = [jnp.int32(0)]
    fresh_starts = [jnp.int32(0)]
    for s in range(SEQS):
        cache_starts.append(cache_starts[s] + prefix_ref[s])
        fresh_starts.append(fresh_starts[s] + ((ends[s] - starts[s] + PAGE - 1) >> 4))

    def pick(token, values):
        result = jnp.full(token.shape, values[0], jnp.int32)
        for s in range(1, SEQS):
            result = jnp.where(token >= starts[s], values[s], result)
        return result

    row = lax.broadcasted_iota(jnp.int32, (8, 128), 0)
    lane = lax.broadcasted_iota(jnp.int32, (8, 128), 1)
    physical = row * 128 + lane
    page = physical >> 4
    slot = jnp.zeros((8, 128), jnp.int32)
    for i in range(order_ref.shape[0]):
        slot = jnp.where(page == order_ref[i], i * PAGE, slot)
    slot = slot + (physical & (PAGE - 1))
    slot_owner = jnp.zeros((8, 128), jnp.int32)
    for s in range(1, SEQS):
        slot_owner = slot_owner + (slot >= cache_starts[s] * PAGE).astype(jnp.int32)

    yy, cc, dx = row & 1, row >> 1, lane >> 5
    holder = ((y + yy) & 1) * 8 + ((x - dx) & 3) * 2 + ((c + cc) & 1)
    token = holder * BLOCK + (lane & (BLOCK - 1))
    token_owner = pick(token, list(range(SEQS)))
    in_prompt = token - pick(token, starts)
    page_slot = pick(token, fresh_starts[:SEQS]) + (in_prompt >> 4)
    fresh_page = jnp.zeros((8, 128), jnp.int32)
    for i in range(fresh_ref.shape[0]):
        fresh_page = jnp.where(page_slot == i, fresh_ref[i], fresh_page)
    target_ref[...] = fresh_page * PAGE + (in_prompt & (PAGE - 1))

    base = [cache_starts[s + 1] * PAGE - starts[s] for s in range(SEQS)]
    for b in range(8):
        at = ((y + b // 4) & 1) * 8 + ((x - b % 4) & 3) * 2 + c
        query = at * BLOCK + lax.broadcasted_iota(jnp.int32, (BLOCK, 128), 0)
        owner = pick(query, list(range(SEQS)))
        reach = pick(query, base) + query
        rows = slice(b * BLOCK, (b + 1) * BLOCK)
        for k in range(6):
            apart = (reach - slot[k : k + 1, :]).astype(jnp.float32)
            dist_ref[rows, k * 128 : (k + 1) * 128] = jnp.where(
                owner == slot_owner[k : k + 1, :], apart, FAR
            )
        for k in range(4):
            gap = query - token[k : k + 1, :]
            usable = (owner == token_owner[k : k + 1, :]) & (gap >= 0)
            dist_ref[rows, (6 + k) * 128 : (7 + k) * 128] = jnp.where(
                usable, gap.astype(jnp.float32), FAR
            )


def layout_tables(segment_ids, prefix_pages, page_order, fresh_order):
    smem = pl.BlockSpec(memory_space=pltpu.SMEM)
    vmem = pl.BlockSpec(memory_space=pltpu.VMEM)
    return pl.pallas_call(
        layout_kernel,
        out_shape=(
            jax.ShapeDtypeStruct((256, 1280), jnp.float32),
            jax.ShapeDtypeStruct((8, 128), jnp.int32),
        ),
        in_specs=[vmem, smem, smem, smem],
        out_specs=(vmem, vmem),
        cost_estimate=pl.CostEstimate(flops=0, bytes_accessed=4_000_000, transcendentals=0),
        name="layout",
    )(segment_ids.reshape(4, 128), prefix_pages, page_order, fresh_order)


def project_kernel(a_ref, b_ref, c_ref, d_ref, gain_ref, mine_ref, other_ref, q_ref, kv_ref, normed, total):
    step = pl.program_id(0)
    depth = mine_ref.shape[0]

    @pl.when(step == 0)
    def _():
        gain = gain_ref[...].astype(jnp.float32)
        for i, ref in enumerate((a_ref, b_ref, c_ref, d_ref)):
            for h in range(2):
                rows = slice(h * 16, (h + 1) * 16)
                values = ref[rows, :].astype(jnp.float32)
                center = values - jnp.mean(values, axis=-1, keepdims=True)
                spread = jnp.mean(center * center, axis=-1, keepdims=True)
                result = (center * lax.rsqrt(spread + 1e-05) * gain).astype(jnp.bfloat16)
                for k in range(normed.shape[0]):
                    normed[k, i * BLOCK + h * 16 : i * BLOCK + (h + 1) * 16, :] = result[
                        :, k * depth : (k + 1) * depth
                    ]
        total[...] = jnp.zeros_like(total)

    left = normed[step]
    total[:, :384] += jnp.dot(left, mine_ref[...], preferred_element_type=jnp.float32)
    total[:, 384:] += jnp.dot(left, other_ref[...], preferred_element_type=jnp.float32)

    @pl.when(step == pl.num_programs(0) - 1)
    def _():
        done = total[...].astype(jnp.bfloat16)
        q_ref[:, :128] = done[:, :128]
        q_ref[:, 128:] = done[:, 384:512]
        kv_ref[:, :256] = done[:, 128:384]
        kv_ref[:, 256:] = done[:, 512:]


def project(pieces, gain, mine, other):
    steps = 4
    depth = mine.shape[0] // steps
    whole = lambda shape: pl.BlockSpec(shape, lambda k: (0, 0))
    return pl.pallas_call(
        project_kernel,
        grid=(steps,),
        out_shape=(
            jax.ShapeDtypeStruct((128, 256), jnp.bfloat16),
            jax.ShapeDtypeStruct((128, 512), jnp.bfloat16),
        ),
        in_specs=[whole((BLOCK, 4096))] * 4
        + [whole((1, 4096))]
        + [pl.BlockSpec((depth, 384), lambda k: (k, 0))] * 2,
        out_specs=(whole((128, 256)), whole((128, 512))),
        scratch_shapes=[
            pltpu.VMEM((steps, 128, depth), jnp.bfloat16),
            pltpu.VMEM((128, 768), jnp.float32),
        ],
        compiler_params=pltpu.CompilerParams(dimension_semantics=("arbitrary",)),
        cost_estimate=pl.CostEstimate(
            flops=2 * 128 * 4096 * 768, bytes_accessed=7_500_000, transcendentals=0
        ),
        name="project",
    )(*pieces, gain.reshape(1, 4096), mine, other)


def attend_kernel(
    qa_ref, qb_ref, kva_ref, kvb_ref, kvc_ref, kvd_ref, mine_ref, other_ref, dist_ref,
    out_mine_ref, out_other_ref, *rest,
):
    out_refs, (scores, weights, queries, context) = rest[:8], rest[8:]
    y, x, c = my_place()
    cached = (mine_ref, other_ref)
    for head in range(2):
        columns = slice(head * HEAD, (head + 1) * HEAD)
        at = (y * 8 + x * 2 + (c ^ head) + 1).astype(jnp.float32)
        slope = jnp.exp2(jnp.full((1, 128), -8.0 * (MODEL_HEADS // N_TP) / MODEL_HEADS, jnp.float32) * at)
        queries[:128, :] = qa_ref[:, columns]
        queries[128:, :] = qb_ref[:, columns]
        q = queries[...]
        near, far = slice(head * 256, head * 256 + 128), slice(head * 256 + 128, head * 256 + 256)
        away = slice((1 - head) * 256, (1 - head) * 256 + 128)
        away_v = slice((1 - head) * 256 + 128, (1 - head) * 256 + 256)
        new = ((kva_ref, near, far), (kvb_ref, near, far), (kvc_ref, away, away_v), (kvd_ref, away, away_v))
        turned = (((1,), (1,)), ((), ()))
        scores[:, :768] = lax.dot_general(
            q, cached[head][0, 0].reshape(768, HEAD), turned, preferred_element_type=jnp.float32
        )
        for i, (ref, keys, _) in enumerate(new):
            scores[:, 768 + i * 128 : 896 + i * 128] = lax.dot_general(
                q, ref[:, keys], turned, preferred_element_type=jnp.float32
            )
        sums = []
        for b in range(8):
            rows = slice(b * BLOCK, (b + 1) * BLOCK)
            pieces = []
            peak = None
            for k in range(10):
                lanes = slice(k * 128, (k + 1) * 128)
                piece = scores[rows, lanes] * HEAD ** (-0.5) - slope * dist_ref[rows, lanes]
                peak = piece if peak is None else jnp.maximum(peak, piece)
                pieces.append(piece)
            peak = jnp.max(peak, axis=1, keepdims=True)
            total = None
            for k in range(10):
                weight = jnp.exp(pieces[k] - peak)
                total = weight if total is None else total + weight
                weights[rows, k * 128 : (k + 1) * 128] = weight.astype(jnp.bfloat16)
            sums.append(jnp.sum(total, axis=1, keepdims=True))
        result = jnp.dot(
            weights[:, :768], cached[head][1, 0].reshape(768, HEAD), preferred_element_type=jnp.float32
        )
        for i, (ref, _, values) in enumerate(new):
            result = result + jnp.dot(
                weights[:, 768 + i * 128 : 896 + i * 128], ref[:, values], preferred_element_type=jnp.float32
            )
        for b in range(8):
            context[b * BLOCK : (b + 1) * BLOCK, columns] = (
                result[b * BLOCK : (b + 1) * BLOCK] / sums[b]
            ).astype(jnp.bfloat16)
    left, right = context[:, :HEAD], context[:, HEAD:]
    for n in range(8):
        lanes = slice(n * 512, (n + 1) * 512)
        partial = (
            jnp.dot(left, out_mine_ref[:, lanes], preferred_element_type=jnp.float32)
            + jnp.dot(right, out_other_ref[:, lanes], preferred_element_type=jnp.float32)
        ).astype(jnp.bfloat16)
        for b in range(8):
            out_refs[b][:, lanes] = partial[b * BLOCK : (b + 1) * BLOCK]


def attend(queries, pairs, mine, other, dist, out_mine, out_other):
    vmem = pl.BlockSpec(memory_space=pltpu.VMEM)
    return pl.pallas_call(
        attend_kernel,
        out_shape=[jax.ShapeDtypeStruct((BLOCK, 4096), jnp.bfloat16)] * 8,
        in_specs=[vmem] * 11,
        out_specs=[vmem] * 8,
        scratch_shapes=[
            pltpu.VMEM((256, 1280), jnp.float32),
            pltpu.VMEM((256, 1280), jnp.bfloat16),
            pltpu.VMEM((256, HEAD), jnp.bfloat16),
            pltpu.VMEM((256, 256), jnp.bfloat16),
        ],
        cost_estimate=pl.CostEstimate(
            flops=4 * 256 * 1280 * 256 + 2 * 256 * 256 * 4096,
            bytes_accessed=7_000_000,
            transcendentals=2 * 256 * 1280,
        ),
        name="attend",
    )(*queries, *pairs, mine, other, dist, out_mine, out_other)


def fresh_kernel(target_ref, kva_ref, kvb_ref, kvc_ref, kvd_ref, out_ref):
    total = out_ref.shape[1]
    places = lax.broadcasted_iota(jnp.int32, (total, 128), 0)
    result = None
    for i, ref in enumerate((kva_ref, kvb_ref, kvc_ref, kvd_ref)):
        columns = slice(0, 256) if i < 2 else slice(256, 512)
        chosen = (places == target_ref[i : i + 1, :]).astype(jnp.float32).astype(jnp.bfloat16)
        part = jnp.dot(chosen, ref[:, columns], preferred_element_type=jnp.float32)
        result = part if result is None else result + part
    out_ref[0] = result[:, :HEAD].astype(jnp.bfloat16)
    out_ref[1] = result[:, HEAD:].astype(jnp.bfloat16)


def fresh(target, pairs, pages):
    vmem = pl.BlockSpec(memory_space=pltpu.VMEM)
    return pl.pallas_call(
        fresh_kernel,
        out_shape=jax.ShapeDtypeStruct((2, pages * PAGE, HEAD), jnp.bfloat16),
        in_specs=[vmem] * 5,
        out_specs=vmem,
        cost_estimate=pl.CostEstimate(
            flops=2 * 640 * 512 * 256, bytes_accessed=2_000_000, transcendentals=0
        ),
        name="fresh",
    )(target, *pairs)


def body(
    tokens,
    norm_gain,
    qkv_weight,
    out_weight,
    segment_ids,
    prefix_pages,
    page_order,
    fresh_order,
    cache_pool,
):
    partner = moved(tokens, 1, 0, 0)
    own = [tokens]
    for dx in (1, 2, 3):
        own.append(moved(tokens, 0, dx, 0))
    qkv_other = moved(qkv_weight, 0, 0, 1)
    out_other = moved(out_weight, 0, 0, 1)
    cache_other = moved(cache_pool, 0, 0, 1)
    across = [partner]
    for dx in (1, 2, 3):
        across.append(moved(partner, 0, dx, 0))
    dist, target = layout_tables(segment_ids, prefix_pages, page_order, fresh_order)
    q_own, kv_own = project(own, norm_gain, qkv_weight, qkv_other)
    kv_own_other = moved(kv_own, 0, 0, 1)
    q_across, kv_across = project(across, norm_gain, qkv_weight, qkv_other)
    kv_across_other = moved(kv_across, 0, 0, 1)
    pairs = (kv_own, kv_across, kv_own_other, kv_across_other)
    partial = attend((q_own, q_across), pairs, cache_pool, cache_other, dist, out_weight, out_other)
    kept, passed = partial[:4], partial[4:]
    passed_in, kept_in = [], []
    for dx in (2, 1, 3):
        passed_in.append(moved(passed[dx], 0, -dx, 0))
    for dx in (2, 1, 3):
        kept_in.append(moved(kept[dx], 0, -dx, 0))

    def added(first, others):
        total = first.astype(jnp.float32)
        for other in others:
            total = total + other.astype(jnp.float32)
        return total

    passed_sum = added(passed[0], passed_in).astype(jnp.bfloat16)
    from_partner = moved(passed_sum, 1, 0, 0)
    fresh_pages = fresh(target, pairs, fresh_order.shape[0])
    summed = added(kept[0], kept_in + [from_partner]).astype(jnp.bfloat16)
    return (summed, fresh_pages.reshape(2, 1, fresh_order.shape[0], PAGE, HEAD))


def solution(mesh):
    placed = (
        P(("req", "tp"), None),
        P(),
        P(None, "tp"),
        P("tp", None),
        P("req"),
        P("req"),
        P("req"),
        P("req"),
        P(None, "tp", "req", None, None),
    )
    return jax.shard_map(
        body,
        mesh=mesh,
        in_specs=placed,
        out_specs=(P(("req", "tp"), None), P(None, "tp", "req", None, None)),
        check_vma=False,
    )
```

```python
import jax
import jax.numpy as jnp
from jax import lax
from jax.experimental import pallas as pl
from jax.experimental.pallas import tpu as pltpu
from jax.sharding import PartitionSpec as P


MODEL_HEADS = 32
N_X = 4
N_TP = 16
BLOCK = 32
PAGE = 16
SEQS = 8
HEAD = 128
FAR = 3e32


def tp_of(y, x, c):
    return (y % 2) * 8 + (x % N_X) * 2 + c % 2


def moved(value, dy, dx, dc):
    pairs = [
        (tp_of(y, x, c), tp_of(y + dy, x + dx, c + dc))
        for y in range(2)
        for x in range(N_X)
        for c in range(2)
    ]
    return lax.ppermute(value, "tp", pairs)


def my_place():
    me = lax.axis_index("tp")
    return me >> 3, (me >> 1) & 3, me & 1


def layout_kernel(*refs):
    sources, (dist_ref, target_ref), held = refs[:7], refs[7:9], refs[9:16]
    sems = refs[16]
    copies = [
        pltpu.make_async_copy(source, place, sems.at[i])
        for i, (source, place) in enumerate(zip(sources, held[3:] + held[:3]))
    ]
    for copy in copies:
        copy.start()
    seg_ref, prefix_ref, order_ref, fresh_ref = held[3:]
    for copy in copies[:4]:
        copy.wait()
    y, x, c = my_place()
    seg = seg_ref[...]
    starts = [jnp.int32(0)]
    for s in range(1, SEQS):
        starts.append(jnp.sum((seg < s).astype(jnp.float32)).astype(jnp.int32))
    ends = starts[1:] + [jnp.int32(seg.shape[0] * seg.shape[1])]
    cache_starts = [jnp.int32(0)]
    fresh_starts = [jnp.int32(0)]
    for s in range(SEQS):
        cache_starts.append(cache_starts[s] + prefix_ref[s])
        fresh_starts.append(fresh_starts[s] + ((ends[s] - starts[s] + PAGE - 1) >> 4))

    def pick(token, values):
        result = jnp.full(token.shape, values[0], jnp.int32)
        for s in range(1, SEQS):
            result = jnp.where(token >= starts[s], values[s], result)
        return result

    row = lax.broadcasted_iota(jnp.int32, (8, 128), 0)
    lane = lax.broadcasted_iota(jnp.int32, (8, 128), 1)
    physical = row * 128 + lane
    page = physical >> 4
    slot = jnp.zeros((8, 128), jnp.int32)
    for i in range(order_ref.shape[0]):
        slot = jnp.where(page == order_ref[i], i * PAGE, slot)
    slot = slot + (physical & (PAGE - 1))
    slot_owner = jnp.zeros((8, 128), jnp.int32)
    for s in range(1, SEQS):
        slot_owner = slot_owner + (slot >= cache_starts[s] * PAGE).astype(jnp.int32)

    yy, cc, dx = row & 1, row >> 1, lane >> 5
    holder = ((y + yy) & 1) * 8 + ((x - dx) & 3) * 2 + ((c + cc) & 1)
    token = holder * BLOCK + (lane & (BLOCK - 1))
    token_owner = pick(token, list(range(SEQS)))
    in_prompt = token - pick(token, starts)
    page_slot = pick(token, fresh_starts[:SEQS]) + (in_prompt >> 4)
    fresh_page = jnp.zeros((8, 128), jnp.int32)
    for i in range(fresh_ref.shape[0]):
        fresh_page = jnp.where(page_slot == i, fresh_ref[i], fresh_page)
    target_ref[...] = fresh_page * PAGE + (in_prompt & (PAGE - 1))

    base = [cache_starts[s + 1] * PAGE - starts[s] for s in range(SEQS)]
    for b in range(8):
        at = ((y + b // 4) & 1) * 8 + ((x - b % 4) & 3) * 2 + c
        query = at * BLOCK + lax.broadcasted_iota(jnp.int32, (BLOCK, 128), 0)
        owner = pick(query, list(range(SEQS)))
        reach = pick(query, base) + query
        rows = slice(b * BLOCK, (b + 1) * BLOCK)
        for k in range(6):
            apart = (reach - slot[k : k + 1, :]).astype(jnp.float32)
            dist_ref[rows, k * 128 : (k + 1) * 128] = jnp.where(
                owner == slot_owner[k : k + 1, :], apart, FAR
            )
        for k in range(4):
            gap = query - token[k : k + 1, :]
            usable = (owner == token_owner[k : k + 1, :]) & (gap >= 0)
            dist_ref[rows, (6 + k) * 128 : (7 + k) * 128] = jnp.where(
                usable, gap.astype(jnp.float32), FAR
            )
    for copy in copies[4:]:
        copy.wait()


def in_vmem(value):
    return pltpu.with_memory_space_constraint(value, pltpu.VMEM)


def in_hbm(value):
    return pltpu.with_memory_space_constraint(value, pltpu.HBM)


def layout_tables(segment_ids, prefix_pages, page_order, fresh_order, gain, tokens, weight):
    vmem = pl.BlockSpec(memory_space=pltpu.VMEM)
    kept = (gain, tokens, weight)
    small = (prefix_pages, page_order, fresh_order)
    return pl.pallas_call(
        layout_kernel,
        out_shape=[
            jax.ShapeDtypeStruct((256, 1280), jnp.float32),
            jax.ShapeDtypeStruct((8, 128), jnp.int32),
        ]
        + [jax.ShapeDtypeStruct(value.shape, value.dtype) for value in kept],
        in_specs=[pl.BlockSpec(memory_space=pltpu.HBM)] * 7,
        out_specs=[vmem] * 5,
        scratch_shapes=[pltpu.VMEM((4, 128), jnp.int32)]
        + [pltpu.SMEM(value.shape, jnp.int32) for value in small]
        + [pltpu.SemaphoreType.DMA((7,))],
        compiler_params=pltpu.CompilerParams(vmem_limit_bytes=12 * 2**20),
        cost_estimate=pl.CostEstimate(flops=0, bytes_accessed=6_000_000, transcendentals=0),
        name="layout",
    )(*[in_hbm(value) for value in (segment_ids.reshape(4, 128), *small, *kept)])


def project_kernel(*refs):
    pieces, (gain_ref, mine_ref, other_ref, q_ref, kv_ref, normed) = refs[:8], refs[8:]
    gain = jnp.concatenate([gain_ref[k : k + 1, :] for k in range(gain_ref.shape[0])], axis=1)
    gain = gain.astype(jnp.float32)
    for i, ref in enumerate(pieces):
        for h in range(2):
            values = ref[h * 16 : (h + 1) * 16, :].astype(jnp.float32)
            center = values - jnp.mean(values, axis=-1, keepdims=True)
            spread = jnp.mean(center * center, axis=-1, keepdims=True)
            normed[i * BLOCK + h * 16 : i * BLOCK + (h + 1) * 16, :] = (
                center * lax.rsqrt(spread + 1e-05) * gain
            ).astype(jnp.bfloat16)
    left = normed[...]

    def times(right):
        return jnp.dot(left, right, preferred_element_type=jnp.float32).astype(jnp.bfloat16)

    first = times(mine_ref[:, :256])
    q_ref[:, :128] = first[:, :128]
    kv_ref[:, :128] = first[:, 128:]
    middle = times(jnp.concatenate([mine_ref[:, 256:], other_ref[:, :128]], axis=1))
    kv_ref[:, 128:256] = middle[:, :128]
    q_ref[:, 128:] = middle[:, 128:]
    kv_ref[:, 256:] = times(other_ref[:, 128:])


def project(pieces, gain, mine, other):
    vmem = pl.BlockSpec(memory_space=pltpu.VMEM)
    return pl.pallas_call(
        project_kernel,
        out_shape=(
            jax.ShapeDtypeStruct((256, 256), jnp.bfloat16),
            jax.ShapeDtypeStruct((256, 512), jnp.bfloat16),
        ),
        in_specs=[vmem] * 11,
        out_specs=(vmem, vmem),
        scratch_shapes=[pltpu.VMEM((256, 4096), jnp.bfloat16)],
        compiler_params=pltpu.CompilerParams(vmem_limit_bytes=24 * 2**20),
        cost_estimate=pl.CostEstimate(
            flops=2 * 256 * 4096 * 768, bytes_accessed=9_000_000, transcendentals=0
        ),
        name="project",
    )(*[in_vmem(piece) for piece in pieces], in_vmem(gain), in_vmem(mine), in_vmem(other))


def out_rows(left, right, mine_ref, other_ref, out_refs):
    for n in range(8):
        lanes = slice(n * 512, (n + 1) * 512)
        partial = (
            jnp.dot(left, mine_ref[:, lanes], preferred_element_type=jnp.float32)
            + jnp.dot(right, other_ref[:, lanes], preferred_element_type=jnp.float32)
        ).astype(jnp.bfloat16)
        for i, out_ref in enumerate(out_refs):
            out_ref[:, lanes] = partial[i * BLOCK : (i + 1) * BLOCK]


def attend_kernel(
    q_ref, near_ref, mine_ref, dist_ref, away_ref, other_ref, out_mine_ref, out_other_ref, *rest,
):
    out_refs, (scores, weights, context_ref) = rest[:8], rest[8:]
    y, x, c = my_place()
    cached = (mine_ref, other_ref)
    turned = (((1,), (1,)), ((), ()))
    log2e = 1.4426950408889634
    for head in range(2):
        columns = slice(head * HEAD, (head + 1) * HEAD)
        at = (y * 8 + x * 2 + (c ^ head) + 1).astype(jnp.float32)
        slope = log2e * jnp.exp2(
            jnp.full((1, 128), -8.0 * (MODEL_HEADS // N_TP) / MODEL_HEADS, jnp.float32) * at
        )
        q = q_ref[:, columns]
        new = ((near_ref, head * 256), (away_ref, (1 - head) * 256))
        scores[:, :768] = lax.dot_general(
            q, cached[head][0, 0].reshape(768, HEAD), turned, preferred_element_type=jnp.float32
        )
        for i, (ref, first) in enumerate(new):
            scores[:, 768 + i * 256 : 1024 + i * 256] = lax.dot_general(
                q, ref[:, first : first + HEAD], turned, preferred_element_type=jnp.float32
            )
        sums = []
        for b in range(8):
            rows = slice(b * BLOCK, (b + 1) * BLOCK)
            pieces = []
            peak = None
            for k in range(10):
                lanes = slice(k * 128, (k + 1) * 128)
                piece = scores[rows, lanes] * (log2e * HEAD ** (-0.5)) - slope * dist_ref[rows, lanes]
                peak = piece if peak is None else jnp.maximum(peak, piece)
                pieces.append(piece)
            peak = jnp.max(peak, axis=1, keepdims=True)
            total = None
            for k in range(10):
                weight = jnp.exp2(pieces[k] - peak)
                total = weight if total is None else total + weight
                weights[rows, k * 128 : (k + 1) * 128] = weight.astype(jnp.bfloat16)
            sums.append(jnp.sum(total, axis=1, keepdims=True))
        result = jnp.dot(
            weights[:, :768], cached[head][1, 0].reshape(768, HEAD), preferred_element_type=jnp.float32
        )
        for i, (ref, first) in enumerate(new):
            result = result + jnp.dot(
                weights[:, 768 + i * 256 : 1024 + i * 256],
                ref[:, first + HEAD : first + 2 * HEAD],
                preferred_element_type=jnp.float32,
            )
        for b in range(8):
            context_ref[b * BLOCK : (b + 1) * BLOCK, columns] = (
                result[b * BLOCK : (b + 1) * BLOCK] / sums[b]
            ).astype(jnp.bfloat16)
    out_rows(context_ref[:, :HEAD], context_ref[:, HEAD:], out_mine_ref, out_other_ref, out_refs)


def attend(queries, near, away, mine, other, dist, out_mine, out_other):
    vmem = pl.BlockSpec(memory_space=pltpu.VMEM)
    operands = (queries, near, mine, dist, away, other, out_mine, out_other)
    return pl.pallas_call(
        attend_kernel,
        out_shape=[jax.ShapeDtypeStruct((BLOCK, 4096), jnp.bfloat16)] * 8,
        in_specs=[vmem] * 8,
        out_specs=[vmem] * 8,
        scratch_shapes=[
            pltpu.VMEM((256, 1280), jnp.float32),
            pltpu.VMEM((256, 1280), jnp.bfloat16),
            pltpu.VMEM((256, 256), jnp.bfloat16),
        ],
        compiler_params=pltpu.CompilerParams(vmem_limit_bytes=24 * 2**20),
        cost_estimate=pl.CostEstimate(
            flops=4 * 256 * 1280 * 256 + 2 * 256 * 256 * 4096,
            bytes_accessed=8_000_000,
            transcendentals=2 * 256 * 1280,
        ),
        name="attend",
    )(*[in_vmem(operand) for operand in operands])


def fresh_kernel(target_ref, near_ref, away_ref, out_ref):
    total = out_ref.shape[1]
    places = lax.broadcasted_iota(jnp.int32, (total, 128), 0)
    result = None
    for i in range(4):
        rows = slice((i & 1) * 128, (i & 1) * 128 + 128)
        piece = near_ref[rows, :256] if i < 2 else away_ref[rows, 256:]
        chosen = (places == target_ref[i : i + 1, :]).astype(jnp.float32).astype(jnp.bfloat16)
        part = jnp.dot(chosen, piece, preferred_element_type=jnp.float32)
        result = part if result is None else result + part
    out_ref[0] = result[:, :HEAD].astype(jnp.bfloat16)
    out_ref[1] = result[:, HEAD:].astype(jnp.bfloat16)


def fresh(target, near, away, pages):
    vmem = pl.BlockSpec(memory_space=pltpu.VMEM)
    return pl.pallas_call(
        fresh_kernel,
        out_shape=jax.ShapeDtypeStruct((2, pages * PAGE, HEAD), jnp.bfloat16),
        in_specs=[vmem] * 3,
        out_specs=vmem,
        compiler_params=pltpu.CompilerParams(vmem_limit_bytes=12 * 2**20),
        cost_estimate=pl.CostEstimate(
            flops=2 * 640 * 512 * 256, bytes_accessed=2_000_000, transcendentals=0
        ),
        name="fresh",
    )(target, near, away)


def body(
    tokens,
    norm_gain,
    qkv_weight,
    out_weight,
    segment_ids,
    prefix_pages,
    page_order,
    fresh_order,
    cache_pool,
):
    def added(values):
        total = values[0].astype(jnp.float32)
        for value in values[1:]:
            total = total + value.astype(jnp.float32)
        return total

    partner = moved(tokens, 1, 0, 0)
    qkv_other = moved(qkv_weight, 0, 0, 1)
    cache_other = moved(cache_pool, 0, 0, 1)
    out_other = moved(out_weight, 0, 0, 1)
    own, across = [tokens], [partner]
    for dx in (1, 2, 3):
        own.append(moved(tokens, 0, dx, 0))
        across.append(moved(partner, 0, dx, 0))
    dist, target, gain, own[0], qkv_mine = layout_tables(
        segment_ids, prefix_pages, page_order, fresh_order,
        norm_gain.reshape(32, 128), tokens, qkv_weight,
    )
    queries, near = project(own + across, gain, qkv_mine, qkv_other)
    away = moved(near, 0, 0, 1)
    partial = attend(queries, near, away, cache_pool, cache_other, dist, out_weight, out_other)
    kept, passed = partial[:4], partial[4:]
    passed_in = [passed[0]]
    for dx in (1, 2, 3):
        passed_in.append(moved(passed[dx], 0, -dx, 0))
    kept_in = [kept[0]]
    for dx in (1, 2, 3):
        kept_in.append(moved(kept[dx], 0, -dx, 0))
    passed_sum = added(passed_in).astype(jnp.bfloat16)
    from_partner = moved(passed_sum, 1, 0, 0)
    fresh_pages = fresh(target, near, away, fresh_order.shape[0])
    kept_sum = lax.optimization_barrier(added([kept_in[0], kept_in[1], kept_in[3]]))
    summed = added([kept_sum, kept_in[2], from_partner]).astype(jnp.bfloat16)
    return (summed, fresh_pages.reshape(2, 1, fresh_order.shape[0], PAGE, HEAD))


def solution(mesh):
    placed = (
        P(("req", "tp"), None),
        P(),
        P(None, "tp"),
        P("tp", None),
        P("req"),
        P("req"),
        P("req"),
        P("req"),
        P(None, "tp", "req", None, None),
    )
    return jax.shard_map(
        body,
        mesh=mesh,
        in_specs=placed,
        out_specs=(P(("req", "tp"), None), P(None, "tp", "req", None, None)),
        check_vma=False,
    )
```

```python
import functools

import jax
import jax.numpy as jnp
from jax import lax
from jax.experimental import pallas as pl
from jax.experimental.pallas import tpu as pltpu
from jax.sharding import PartitionSpec as P


MODEL_HEADS = 32
N_X = 4
N_TP = 16
BLOCK = 32
PAGE = 16
SEQS = 8
HEAD = 128
FAR = 3e32


def tp_of(y, x, c):
    return (y % 2) * 8 + (x % N_X) * 2 + c % 2


def moved(value, dy, dx, dc):
    pairs = [
        (tp_of(y, x, c), tp_of(y + dy, x + dx, c + dc))
        for y in range(2)
        for x in range(N_X)
        for c in range(2)
    ]
    return lax.ppermute(value, "tp", pairs)


def along_x(value):
    groups = [[tp_of(y, x, c) for x in range(N_X)] for y in range(2) for c in range(2)]
    return lax.all_to_all(value, "tp", 0, 0, axis_index_groups=groups)


def my_place():
    me = lax.axis_index("tp")
    return me >> 3, (me >> 1) & 3, me & 1


def layout_kernel(*refs):
    sources, (dist_ref, target_ref), held = refs[:7], refs[7:9], refs[9:16]
    sems = refs[16]
    copies = [
        pltpu.make_async_copy(source, place, sems.at[i])
        for i, (source, place) in enumerate(zip(sources, held[3:] + held[:3]))
    ]
    for copy in copies:
        copy.start()
    seg_ref, prefix_ref, order_ref, fresh_ref = held[3:]
    for copy in copies[:4]:
        copy.wait()
    y, x, c = my_place()
    seg = seg_ref[...]
    starts = [jnp.int32(0)]
    for s in range(1, SEQS):
        starts.append(jnp.sum((seg < s).astype(jnp.float32)).astype(jnp.int32))
    ends = starts[1:] + [jnp.int32(seg.shape[0] * seg.shape[1])]
    cache_starts = [jnp.int32(0)]
    fresh_starts = [jnp.int32(0)]
    for s in range(SEQS):
        cache_starts.append(cache_starts[s] + prefix_ref[s])
        fresh_starts.append(fresh_starts[s] + ((ends[s] - starts[s] + PAGE - 1) >> 4))

    def pick(token, values):
        result = jnp.full(token.shape, values[0], jnp.int32)
        for s in range(1, SEQS):
            result = jnp.where(token >= starts[s], values[s], result)
        return result

    row = lax.broadcasted_iota(jnp.int32, (8, 128), 0)
    lane = lax.broadcasted_iota(jnp.int32, (8, 128), 1)
    physical = row * 128 + lane
    page = physical >> 4
    slot = jnp.zeros((8, 128), jnp.int32)
    for i in range(order_ref.shape[0]):
        slot = jnp.where(page == order_ref[i], i * PAGE, slot)
    slot = slot + (physical & (PAGE - 1))
    slot_owner = jnp.zeros((8, 128), jnp.int32)
    for s in range(1, SEQS):
        slot_owner = slot_owner + (slot >= cache_starts[s] * PAGE).astype(jnp.int32)

    yy, cc, dx = row & 1, row >> 1, lane >> 5
    holder = ((y + yy) & 1) * 8 + ((x - dx) & 3) * 2 + ((c + cc) & 1)
    token = holder * BLOCK + (lane & (BLOCK - 1))
    token_owner = pick(token, list(range(SEQS)))
    in_prompt = token - pick(token, starts)
    page_slot = pick(token, fresh_starts[:SEQS]) + (in_prompt >> 4)
    fresh_page = jnp.zeros((8, 128), jnp.int32)
    for i in range(fresh_ref.shape[0]):
        fresh_page = jnp.where(page_slot == i, fresh_ref[i], fresh_page)
    target_ref[...] = fresh_page * PAGE + (in_prompt & (PAGE - 1))

    base = [cache_starts[s + 1] * PAGE - starts[s] for s in range(SEQS)]
    for b in range(8):
        at = ((y + b // 4) & 1) * 8 + ((x - b % 4) & 3) * 2 + c
        query = at * BLOCK + lax.broadcasted_iota(jnp.int32, (BLOCK, 128), 0)
        owner = pick(query, list(range(SEQS)))
        reach = pick(query, base) + query
        rows = slice(b * BLOCK, (b + 1) * BLOCK)
        for k in range(6):
            apart = (reach - slot[k : k + 1, :]).astype(jnp.float32)
            dist_ref[rows, k * 128 : (k + 1) * 128] = jnp.where(
                owner == slot_owner[k : k + 1, :], apart, FAR
            )
        for k in range(4):
            gap = query - token[k : k + 1, :]
            usable = (owner == token_owner[k : k + 1, :]) & (gap >= 0)
            dist_ref[rows, (6 + k) * 128 : (7 + k) * 128] = jnp.where(
                usable, gap.astype(jnp.float32), FAR
            )
    for copy in copies[4:]:
        copy.wait()


def in_vmem(value):
    return pltpu.with_memory_space_constraint(value, pltpu.VMEM)


def in_hbm(value):
    return pltpu.with_memory_space_constraint(value, pltpu.HBM)


def layout_tables(segment_ids, prefix_pages, page_order, fresh_order, gain, tokens, weight):
    vmem = pl.BlockSpec(memory_space=pltpu.VMEM)
    kept = (gain, tokens, weight)
    small = (prefix_pages, page_order, fresh_order)
    return pl.pallas_call(
        layout_kernel,
        out_shape=[
            jax.ShapeDtypeStruct((256, 1280), jnp.float32),
            jax.ShapeDtypeStruct((8, 128), jnp.int32),
        ]
        + [jax.ShapeDtypeStruct(value.shape, value.dtype) for value in kept],
        in_specs=[pl.BlockSpec(memory_space=pltpu.HBM)] * 7,
        out_specs=[vmem] * 5,
        scratch_shapes=[pltpu.VMEM((4, 128), jnp.int32)]
        + [pltpu.SMEM(value.shape, jnp.int32) for value in small]
        + [pltpu.SemaphoreType.DMA((7,))],
        compiler_params=pltpu.CompilerParams(vmem_limit_bytes=12 * 2**20),
        cost_estimate=pl.CostEstimate(flops=0, bytes_accessed=6_000_000, transcendentals=0),
        name="layout",
    )(*[in_hbm(value) for value in (segment_ids.reshape(4, 128), *small, *kept)])


def project_kernel(*refs):
    pieces, (gain_ref, mine_ref, other_ref, normed, kv_ref) = refs[:8], refs[8:]
    gain = jnp.concatenate([gain_ref[k : k + 1, :] for k in range(gain_ref.shape[0])], axis=1)
    gain = gain.astype(jnp.float32)
    for i, ref in enumerate(pieces):
        for h in range(2):
            values = ref[h * 16 : (h + 1) * 16, :].astype(jnp.float32)
            center = values - jnp.mean(values, axis=-1, keepdims=True)
            spread = jnp.mean(center * center, axis=-1, keepdims=True)
            normed[i * BLOCK + h * 16 : i * BLOCK + (h + 1) * 16, :] = (
                center * lax.rsqrt(spread + 1e-05) * gain
            ).astype(jnp.bfloat16)
    left = normed[...]

    def times(right):
        return jnp.dot(left, right, preferred_element_type=jnp.float32).astype(jnp.bfloat16)

    kv_ref[:, :256] = times(mine_ref[:, 128:])
    kv_ref[:, 256:] = times(other_ref[:, 128:])


def query_kernel(normed, mine_ref, other_ref, q_ref):
    both = jnp.concatenate([mine_ref[:, :128], other_ref[:, :128]], axis=1)
    q_ref[...] = jnp.dot(normed[...], both, preferred_element_type=jnp.float32).astype(jnp.bfloat16)


def project(pieces, gain, mine, other):
    vmem = pl.BlockSpec(memory_space=pltpu.VMEM)
    return pl.pallas_call(
        project_kernel,
        out_shape=(
            jax.ShapeDtypeStruct((256, 4096), jnp.bfloat16),
            jax.ShapeDtypeStruct((256, 512), jnp.bfloat16),
        ),
        in_specs=[vmem] * 11,
        out_specs=(vmem, vmem),
        compiler_params=pltpu.CompilerParams(vmem_limit_bytes=24 * 2**20),
        cost_estimate=pl.CostEstimate(
            flops=2 * 256 * 4096 * 512, bytes_accessed=9_000_000, transcendentals=0
        ),
        name="project",
    )(*[in_vmem(piece) for piece in pieces], in_vmem(gain), in_vmem(mine), in_vmem(other))


def query(normed, mine, other):
    vmem = pl.BlockSpec(memory_space=pltpu.VMEM)
    return pl.pallas_call(
        query_kernel,
        out_shape=jax.ShapeDtypeStruct((256, 256), jnp.bfloat16),
        in_specs=[vmem] * 3,
        out_specs=vmem,
        compiler_params=pltpu.CompilerParams(vmem_limit_bytes=24 * 2**20),
        cost_estimate=pl.CostEstimate(
            flops=2 * 256 * 4096 * 256, bytes_accessed=5_000_000, transcendentals=0
        ),
        name="query",
    )(in_vmem(normed), in_vmem(mine), in_vmem(other))


def out_rows(left, right, mine_ref, other_ref, out_refs):
    for n in range(8):
        lanes = slice(n * 512, (n + 1) * 512)
        partial = (
            jnp.dot(left, mine_ref[:, lanes], preferred_element_type=jnp.float32)
            + jnp.dot(right, other_ref[:, lanes], preferred_element_type=jnp.float32)
        ).astype(jnp.bfloat16)
        for i in range(N_X):
            rows = partial[i * BLOCK : (i + 1) * BLOCK]
            if len(out_refs) == 1:
                x = my_place()[1]
                out_refs[0][(x - i) & 3, :, lanes] = rows
            else:
                out_refs[i][:, lanes] = rows


def attend_kernel(
    half, q_ref, near_ref, mine_ref, dist_ref, away_ref, other_ref, out_mine_ref, out_other_ref, *rest,
):
    out_refs, (scores, weights, context_ref) = rest[:-3], rest[-3:]
    mine_rows = slice(half * 128, half * 128 + 128)
    y, x, c = my_place()
    cached = (mine_ref, other_ref)
    turned = (((1,), (1,)), ((), ()))
    log2e = 1.4426950408889634
    for head in range(2):
        columns = slice(head * HEAD, (head + 1) * HEAD)
        at = (y * 8 + x * 2 + (c ^ head) + 1).astype(jnp.float32)
        slope = log2e * jnp.exp2(
            jnp.full((1, 128), -8.0 * (MODEL_HEADS // N_TP) / MODEL_HEADS, jnp.float32) * at
        )
        q = q_ref[mine_rows, columns]
        new = ((near_ref, head * 256), (away_ref, (1 - head) * 256))
        scores[:, :768] = lax.dot_general(
            q, cached[head][0, 0].reshape(768, HEAD), turned, preferred_element_type=jnp.float32
        )
        for i, (ref, first) in enumerate(new):
            scores[:, 768 + i * 256 : 1024 + i * 256] = lax.dot_general(
                q, ref[:, first : first + HEAD], turned, preferred_element_type=jnp.float32
            )
        sums = []
        for b in range(N_X):
            rows = slice(b * BLOCK, (b + 1) * BLOCK)
            table = slice(half * 128 + b * BLOCK, half * 128 + (b + 1) * BLOCK)
            pieces = []
            peak = None
            for k in range(10):
                lanes = slice(k * 128, (k + 1) * 128)
                piece = scores[rows, lanes] * (log2e * HEAD ** (-0.5)) - slope * dist_ref[table, lanes]
                peak = piece if peak is None else jnp.maximum(peak, piece)
                pieces.append(piece)
            peak = jnp.max(peak, axis=1, keepdims=True)
            total = None
            for k in range(10):
                weight = jnp.exp2(pieces[k] - peak)
                total = weight if total is None else total + weight
                weights[rows, k * 128 : (k + 1) * 128] = weight.astype(jnp.bfloat16)
            sums.append(jnp.sum(total, axis=1, keepdims=True))
        result = jnp.dot(
            weights[:, :768], cached[head][1, 0].reshape(768, HEAD), preferred_element_type=jnp.float32
        )
        for i, (ref, first) in enumerate(new):
            result = result + jnp.dot(
                weights[:, 768 + i * 256 : 1024 + i * 256],
                ref[:, first + HEAD : first + 2 * HEAD],
                preferred_element_type=jnp.float32,
            )
        for b in range(N_X):
            context_ref[b * BLOCK : (b + 1) * BLOCK, columns] = (
                result[b * BLOCK : (b + 1) * BLOCK] / sums[b]
            ).astype(jnp.bfloat16)
    out_rows(context_ref[:, :HEAD], context_ref[:, HEAD:], out_mine_ref, out_other_ref, out_refs)


def attend(half, operands):
    vmem = pl.BlockSpec(memory_space=pltpu.VMEM)
    shapes = [jax.ShapeDtypeStruct((BLOCK, 4096), jnp.bfloat16)] * N_X
    if half == 0:
        shapes = [jax.ShapeDtypeStruct((N_X, BLOCK, 4096), jnp.bfloat16)]
    return pl.pallas_call(
        functools.partial(attend_kernel, half),
        out_shape=shapes,
        in_specs=[vmem] * 8,
        out_specs=[vmem] * len(shapes),
        scratch_shapes=[
            pltpu.VMEM((128, 1280), jnp.float32),
            pltpu.VMEM((128, 1280), jnp.bfloat16),
            pltpu.VMEM((128, 256), jnp.bfloat16),
        ],
        compiler_params=pltpu.CompilerParams(vmem_limit_bytes=24 * 2**20),
        cost_estimate=pl.CostEstimate(
            flops=4 * 128 * 1280 * 256 + 2 * 128 * 256 * 4096,
            bytes_accessed=6_000_000,
            transcendentals=2 * 128 * 1280,
        ),
        name="attend",
    )(*operands)


def fresh_kernel(target_ref, near_ref, away_ref, out_ref):
    total = out_ref.shape[1]
    places = lax.broadcasted_iota(jnp.int32, (total, 128), 0)
    result = None
    for i in range(4):
        rows = slice((i & 1) * 128, (i & 1) * 128 + 128)
        piece = near_ref[rows, :256] if i < 2 else away_ref[rows, 256:]
        chosen = (places == target_ref[i : i + 1, :]).astype(jnp.float32).astype(jnp.bfloat16)
        part = jnp.dot(chosen, piece, preferred_element_type=jnp.float32)
        result = part if result is None else result + part
    out_ref[0] = result[:, :HEAD].astype(jnp.bfloat16)
    out_ref[1] = result[:, HEAD:].astype(jnp.bfloat16)


def fresh(target, near, away, pages):
    vmem = pl.BlockSpec(memory_space=pltpu.VMEM)
    return pl.pallas_call(
        fresh_kernel,
        out_shape=jax.ShapeDtypeStruct((2, pages * PAGE, HEAD), jnp.bfloat16),
        in_specs=[vmem] * 3,
        out_specs=vmem,
        compiler_params=pltpu.CompilerParams(vmem_limit_bytes=12 * 2**20),
        cost_estimate=pl.CostEstimate(
            flops=2 * 640 * 512 * 256, bytes_accessed=2_000_000, transcendentals=0
        ),
        name="fresh",
    )(target, near, away)


def body(
    tokens,
    norm_gain,
    qkv_weight,
    out_weight,
    segment_ids,
    prefix_pages,
    page_order,
    fresh_order,
    cache_pool,
):
    def added(values):
        total = values[0].astype(jnp.float32)
        for value in values[1:]:
            total = total + value.astype(jnp.float32)
        return total

    partner = moved(tokens, 1, 0, 0)
    qkv_other = moved(qkv_weight, 0, 0, 1)
    cache_other = moved(cache_pool, 0, 0, 1)
    out_other = moved(out_weight, 0, 0, 1)
    own, across = [tokens], [partner]
    for dx in (1, 2, 3):
        own.append(moved(tokens, 0, dx, 0))
        across.append(moved(partner, 0, dx, 0))
    dist, target, gain, own[0], qkv_mine = layout_tables(
        segment_ids, prefix_pages, page_order, fresh_order,
        norm_gain.reshape(32, 128), tokens, qkv_weight,
    )
    normed, near = project(own + across, gain, qkv_mine, qkv_other)
    away = moved(near, 0, 0, 1)
    queries = query(normed, qkv_mine, qkv_other)
    operands = (queries, near, cache_pool, dist, away, cache_other, out_weight, out_other)
    operands = tuple(in_vmem(operand) for operand in operands)
    passed = attend(1, operands)
    kept = attend(0, operands)
    passed_in = [passed[0]]
    for dx in (1, 2, 3):
        passed_in.append(moved(passed[dx], 0, -dx, 0))
    kept_in = along_x(kept[0])
    passed_sum = added(passed_in).astype(jnp.bfloat16)
    from_partner = moved(passed_sum, 1, 0, 0)
    fresh_pages = fresh(target, near, away, fresh_order.shape[0])
    kept_sum = lax.optimization_barrier(jnp.sum(kept_in.astype(jnp.float32), axis=0))
    summed = added([kept_sum, from_partner]).astype(jnp.bfloat16)
    return (summed, fresh_pages.reshape(2, 1, fresh_order.shape[0], PAGE, HEAD))


def solution(mesh):
    placed = (
        P(("req", "tp"), None),
        P(),
        P(None, "tp"),
        P("tp", None),
        P("req"),
        P("req"),
        P("req"),
        P("req"),
        P(None, "tp", "req", None, None),
    )
    return jax.shard_map(
        body,
        mesh=mesh,
        in_specs=placed,
        out_specs=(P(("req", "tp"), None), P(None, "tp", "req", None, None)),
        check_vma=False,
    )
```

```python
import functools

import jax
import jax.numpy as jnp
from jax import lax
from jax.experimental import pallas as pl
from jax.experimental.pallas import tpu as pltpu
from jax.sharding import PartitionSpec as P


MODEL_HEADS = 32
N_X = 4
N_TP = 16
BLOCK = 32
PAGE = 16
SEQS = 8
HEAD = 128
FAR = 3e32


def tp_of(y, x, c):
    return (y % 2) * 8 + (x % N_X) * 2 + c % 2


def place_of(x, step):
    return ((x ^ (step & 1)) + (step & 2)) & 3


def moved(value, dy, step, dc):
    pairs = [
        (tp_of(y, x, c), tp_of(y + dy, place_of(x, step), c + dc))
        for y in range(2)
        for x in range(N_X)
        for c in range(2)
    ]
    return lax.ppermute(value, "tp", pairs)


def along_x(value):
    groups = [[tp_of(y, x, c) for x in range(N_X)] for y in range(2) for c in range(2)]
    return lax.all_to_all(value, "tp", 0, 0, axis_index_groups=groups)


def my_place():
    me = lax.axis_index("tp")
    return me >> 3, (me >> 1) & 3, me & 1


def layout_kernel(*refs):
    sources, (dist_ref, target_ref), held = refs[:7], refs[7:9], refs[9:16]
    sems = refs[16]
    copies = [
        pltpu.make_async_copy(source, place, sems.at[i])
        for i, (source, place) in enumerate(zip(sources, held[3:] + held[:3]))
    ]
    for copy in copies:
        copy.start()
    seg_ref, prefix_ref, order_ref, fresh_ref = held[3:]
    for copy in copies[:4]:
        copy.wait()
    y, x, c = my_place()
    seg = seg_ref[...]
    starts = [jnp.int32(0)]
    for s in range(1, SEQS):
        starts.append(jnp.sum((seg < s).astype(jnp.float32)).astype(jnp.int32))
    ends = starts[1:] + [jnp.int32(seg.shape[0] * seg.shape[1])]
    cache_starts = [jnp.int32(0)]
    fresh_starts = [jnp.int32(0)]
    for s in range(SEQS):
        cache_starts.append(cache_starts[s] + prefix_ref[s])
        fresh_starts.append(fresh_starts[s] + ((ends[s] - starts[s] + PAGE - 1) >> 4))

    def pick(token, values):
        result = jnp.full(token.shape, values[0], jnp.int32)
        for s in range(1, SEQS):
            result = jnp.where(token >= starts[s], values[s], result)
        return result

    row = lax.broadcasted_iota(jnp.int32, (8, 128), 0)
    lane = lax.broadcasted_iota(jnp.int32, (8, 128), 1)
    physical = row * 128 + lane
    page = physical >> 4
    slot = jnp.zeros((8, 128), jnp.int32)
    for i in range(order_ref.shape[0]):
        slot = jnp.where(page == order_ref[i], i * PAGE, slot)
    slot = slot + (physical & (PAGE - 1))
    slot_owner = jnp.zeros((8, 128), jnp.int32)
    for s in range(1, SEQS):
        slot_owner = slot_owner + (slot >= cache_starts[s] * PAGE).astype(jnp.int32)

    yy, cc, dx = row & 1, row >> 1, lane >> 5
    holder = ((y + yy) & 1) * 8 + place_of(x, dx) * 2 + ((c + cc) & 1)
    token = holder * BLOCK + (lane & (BLOCK - 1))
    token_owner = pick(token, list(range(SEQS)))
    in_prompt = token - pick(token, starts)
    page_slot = pick(token, fresh_starts[:SEQS]) + (in_prompt >> 4)
    fresh_page = jnp.zeros((8, 128), jnp.int32)
    for i in range(fresh_ref.shape[0]):
        fresh_page = jnp.where(page_slot == i, fresh_ref[i], fresh_page)
    target_ref[...] = fresh_page * PAGE + (in_prompt & (PAGE - 1))

    base = [cache_starts[s + 1] * PAGE - starts[s] for s in range(SEQS)]
    for b in range(8):
        at = ((y + b // 4) & 1) * 8 + place_of(x, b % 4) * 2 + c
        query = at * BLOCK + lax.broadcasted_iota(jnp.int32, (BLOCK, 128), 0)
        owner = pick(query, list(range(SEQS)))
        reach = pick(query, base) + query
        rows = slice(b * BLOCK, (b + 1) * BLOCK)
        for k in range(6):
            apart = (reach - slot[k : k + 1, :]).astype(jnp.float32)
            dist_ref[rows, k * 128 : (k + 1) * 128] = jnp.where(
                owner == slot_owner[k : k + 1, :], apart, FAR
            )
        for k in range(4):
            gap = query - token[k : k + 1, :]
            usable = (owner == token_owner[k : k + 1, :]) & (gap >= 0)
            dist_ref[rows, (6 + k) * 128 : (7 + k) * 128] = jnp.where(
                usable, gap.astype(jnp.float32), FAR
            )
    for copy in copies[4:]:
        copy.wait()


def in_vmem(value):
    return pltpu.with_memory_space_constraint(value, pltpu.VMEM)


def in_hbm(value):
    return pltpu.with_memory_space_constraint(value, pltpu.HBM)


def layout_tables(segment_ids, prefix_pages, page_order, fresh_order, gain, tokens, weight):
    vmem = pl.BlockSpec(memory_space=pltpu.VMEM)
    kept = (gain, tokens, weight)
    small = (prefix_pages, page_order, fresh_order)
    return pl.pallas_call(
        layout_kernel,
        out_shape=[
            jax.ShapeDtypeStruct((256, 1280), jnp.float32),
            jax.ShapeDtypeStruct((8, 128), jnp.int32),
        ]
        + [jax.ShapeDtypeStruct(value.shape, value.dtype) for value in kept],
        in_specs=[pl.BlockSpec(memory_space=pltpu.HBM)] * 7,
        out_specs=[vmem] * 5,
        scratch_shapes=[pltpu.VMEM((4, 128), jnp.int32)]
        + [pltpu.SMEM(value.shape, jnp.int32) for value in small]
        + [pltpu.SemaphoreType.DMA((7,))],
        compiler_params=pltpu.CompilerParams(vmem_limit_bytes=12 * 2**20),
        cost_estimate=pl.CostEstimate(flops=0, bytes_accessed=6_000_000, transcendentals=0),
        name="layout",
    )(*[in_hbm(value) for value in (segment_ids.reshape(4, 128), *small, *kept)])


def project_kernel(*refs):
    pieces, (gain_ref, mine_ref, other_ref, normed, kv_ref) = refs[:8], refs[8:]
    gain = jnp.concatenate([gain_ref[k : k + 1, :] for k in range(gain_ref.shape[0])], axis=1)
    gain = gain.astype(jnp.float32)
    for i, ref in enumerate(pieces):
        for h in range(2):
            values = ref[h * 16 : (h + 1) * 16, :].astype(jnp.float32)
            center = values - jnp.mean(values, axis=-1, keepdims=True)
            spread = jnp.mean(center * center, axis=-1, keepdims=True)
            normed[i * BLOCK + h * 16 : i * BLOCK + (h + 1) * 16, :] = (
                center * lax.rsqrt(spread + 1e-05) * gain
            ).astype(jnp.bfloat16)
    left = normed[...]

    def times(right):
        return jnp.dot(left, right, preferred_element_type=jnp.float32).astype(jnp.bfloat16)

    kv_ref[:, :256] = times(mine_ref[:, 128:])
    kv_ref[:, 256:] = times(other_ref[:, 128:])


def query_kernel(normed, mine_ref, other_ref, q_ref):
    both = jnp.concatenate([mine_ref[:, :128], other_ref[:, :128]], axis=1)
    q_ref[...] = jnp.dot(normed[...], both, preferred_element_type=jnp.float32).astype(jnp.bfloat16)


def project(pieces, gain, mine, other):
    vmem = pl.BlockSpec(memory_space=pltpu.VMEM)
    return pl.pallas_call(
        project_kernel,
        out_shape=(
            jax.ShapeDtypeStruct((256, 4096), jnp.bfloat16),
            jax.ShapeDtypeStruct((256, 512), jnp.bfloat16),
        ),
        in_specs=[vmem] * 11,
        out_specs=(vmem, vmem),
        compiler_params=pltpu.CompilerParams(vmem_limit_bytes=24 * 2**20),
        cost_estimate=pl.CostEstimate(
            flops=2 * 256 * 4096 * 512, bytes_accessed=9_000_000, transcendentals=0
        ),
        name="project",
    )(*[in_vmem(piece) for piece in pieces], in_vmem(gain), in_vmem(mine), in_vmem(other))


def query(normed, mine, other):
    vmem = pl.BlockSpec(memory_space=pltpu.VMEM)
    return pl.pallas_call(
        query_kernel,
        out_shape=jax.ShapeDtypeStruct((256, 256), jnp.bfloat16),
        in_specs=[vmem] * 3,
        out_specs=vmem,
        compiler_params=pltpu.CompilerParams(vmem_limit_bytes=24 * 2**20),
        cost_estimate=pl.CostEstimate(
            flops=2 * 256 * 4096 * 256, bytes_accessed=5_000_000, transcendentals=0
        ),
        name="query",
    )(in_vmem(normed), in_vmem(mine), in_vmem(other))


def out_rows(left, right, mine_ref, other_ref, out_refs):
    for n in range(8):
        lanes = slice(n * 512, (n + 1) * 512)
        partial = (
            jnp.dot(left, mine_ref[:, lanes], preferred_element_type=jnp.float32)
            + jnp.dot(right, other_ref[:, lanes], preferred_element_type=jnp.float32)
        ).astype(jnp.bfloat16)
        for i in range(N_X):
            rows = partial[i * BLOCK : (i + 1) * BLOCK]
            if len(out_refs) == 1:
                x = my_place()[1]
                out_refs[0][place_of(x, i), :, lanes] = rows
            else:
                out_refs[i][:, lanes] = rows


def attend_kernel(
    half, q_ref, near_ref, mine_ref, dist_ref, away_ref, other_ref, out_mine_ref, out_other_ref, *rest,
):
    out_refs, (scores, weights, context_ref) = rest[:-3], rest[-3:]
    mine_rows = slice(half * 128, half * 128 + 128)
    y, x, c = my_place()
    cached = (mine_ref, other_ref)
    turned = (((1,), (1,)), ((), ()))
    log2e = 1.4426950408889634
    for head in range(2):
        columns = slice(head * HEAD, (head + 1) * HEAD)
        at = (y * 8 + x * 2 + (c ^ head) + 1).astype(jnp.float32)
        slope = log2e * jnp.exp2(
            jnp.full((1, 128), -8.0 * (MODEL_HEADS // N_TP) / MODEL_HEADS, jnp.float32) * at
        )
        q = q_ref[mine_rows, columns]
        new = ((near_ref, head * 256), (away_ref, (1 - head) * 256))
        scores[:, :768] = lax.dot_general(
            q, cached[head][0, 0].reshape(768, HEAD), turned, preferred_element_type=jnp.float32
        )
        for i, (ref, first) in enumerate(new):
            scores[:, 768 + i * 256 : 1024 + i * 256] = lax.dot_general(
                q, ref[:, first : first + HEAD], turned, preferred_element_type=jnp.float32
            )
        sums = []
        for b in range(N_X):
            rows = slice(b * BLOCK, (b + 1) * BLOCK)
            table = slice(half * 128 + b * BLOCK, half * 128 + (b + 1) * BLOCK)
            pieces = []
            peak = None
            for k in range(10):
                lanes = slice(k * 128, (k + 1) * 128)
                piece = scores[rows, lanes] * (log2e * HEAD ** (-0.5)) - slope * dist_ref[table, lanes]
                peak = piece if peak is None else jnp.maximum(peak, piece)
                pieces.append(piece)
            peak = jnp.max(peak, axis=1, keepdims=True)
            total = None
            for k in range(10):
                weight = jnp.exp2(pieces[k] - peak)
                total = weight if total is None else total + weight
                weights[rows, k * 128 : (k + 1) * 128] = weight.astype(jnp.bfloat16)
            sums.append(jnp.sum(total, axis=1, keepdims=True))
        result = jnp.dot(
            weights[:, :768], cached[head][1, 0].reshape(768, HEAD), preferred_element_type=jnp.float32
        )
        for i, (ref, first) in enumerate(new):
            result = result + jnp.dot(
                weights[:, 768 + i * 256 : 1024 + i * 256],
                ref[:, first + HEAD : first + 2 * HEAD],
                preferred_element_type=jnp.float32,
            )
        for b in range(N_X):
            context_ref[b * BLOCK : (b + 1) * BLOCK, columns] = (
                result[b * BLOCK : (b + 1) * BLOCK] / sums[b]
            ).astype(jnp.bfloat16)
    out_rows(context_ref[:, :HEAD], context_ref[:, HEAD:], out_mine_ref, out_other_ref, out_refs)


def attend(half, operands):
    vmem = pl.BlockSpec(memory_space=pltpu.VMEM)
    shapes = [jax.ShapeDtypeStruct((BLOCK, 4096), jnp.bfloat16)] * N_X
    if half == 0:
        shapes = [jax.ShapeDtypeStruct((N_X, BLOCK, 4096), jnp.bfloat16)]
    return pl.pallas_call(
        functools.partial(attend_kernel, half),
        out_shape=shapes,
        in_specs=[vmem] * 8,
        out_specs=[vmem] * len(shapes),
        scratch_shapes=[
            pltpu.VMEM((128, 1280), jnp.float32),
            pltpu.VMEM((128, 1280), jnp.bfloat16),
            pltpu.VMEM((128, 256), jnp.bfloat16),
        ],
        compiler_params=pltpu.CompilerParams(vmem_limit_bytes=24 * 2**20),
        cost_estimate=pl.CostEstimate(
            flops=4 * 128 * 1280 * 256 + 2 * 128 * 256 * 4096,
            bytes_accessed=6_000_000,
            transcendentals=2 * 128 * 1280,
        ),
        name="attend",
    )(*operands)


def fresh_kernel(target_ref, near_ref, away_ref, out_ref):
    total = out_ref.shape[1]
    places = lax.broadcasted_iota(jnp.int32, (total, 128), 0)
    result = None
    for i in range(4):
        rows = slice((i & 1) * 128, (i & 1) * 128 + 128)
        piece = near_ref[rows, :256] if i < 2 else away_ref[rows, 256:]
        chosen = (places == target_ref[i : i + 1, :]).astype(jnp.float32).astype(jnp.bfloat16)
        part = jnp.dot(chosen, piece, preferred_element_type=jnp.float32)
        result = part if result is None else result + part
    out_ref[0] = result[:, :HEAD].astype(jnp.bfloat16)
    out_ref[1] = result[:, HEAD:].astype(jnp.bfloat16)


def fresh(target, near, away, pages):
    vmem = pl.BlockSpec(memory_space=pltpu.VMEM)
    return pl.pallas_call(
        fresh_kernel,
        out_shape=jax.ShapeDtypeStruct((2, pages * PAGE, HEAD), jnp.bfloat16),
        in_specs=[vmem] * 3,
        out_specs=vmem,
        compiler_params=pltpu.CompilerParams(vmem_limit_bytes=12 * 2**20),
        cost_estimate=pl.CostEstimate(
            flops=2 * 640 * 512 * 256, bytes_accessed=2_000_000, transcendentals=0
        ),
        name="fresh",
    )(target, near, away)


def body(
    tokens,
    norm_gain,
    qkv_weight,
    out_weight,
    segment_ids,
    prefix_pages,
    page_order,
    fresh_order,
    cache_pool,
):
    def added(values):
        total = values[0].astype(jnp.float32)
        for value in values[1:]:
            total = total + value.astype(jnp.float32)
        return total

    partner = moved(tokens, 1, 0, 0)
    qkv_other = moved(qkv_weight, 0, 0, 1)
    cache_other = moved(cache_pool, 0, 0, 1)
    out_other = moved(out_weight, 0, 0, 1)
    own, across = [tokens], [partner]
    for dx in (1, 2, 3):
        own.append(moved(tokens, 0, dx, 0))
        across.append(moved(partner, 0, dx, 0))
    dist, target, gain, own[0], qkv_mine = layout_tables(
        segment_ids, prefix_pages, page_order, fresh_order,
        norm_gain.reshape(32, 128), tokens, qkv_weight,
    )
    normed, near = project(own + across, gain, qkv_mine, qkv_other)
    away = moved(near, 0, 0, 1)
    queries = query(normed, qkv_mine, qkv_other)
    operands = (queries, near, cache_pool, dist, away, cache_other, out_weight, out_other)
    operands = tuple(in_vmem(operand) for operand in operands)
    passed = attend(1, operands)
    kept = attend(0, operands)
    passed_in = [passed[0]]
    for dx in (1, 2, 3):
        passed_in.append(moved(passed[dx], 0, dx, 0))
    kept_in = along_x(kept[0])
    passed_sum = added(passed_in).astype(jnp.bfloat16)
    from_partner = moved(passed_sum, 1, 0, 0)
    fresh_pages = fresh(target, near, away, fresh_order.shape[0])
    kept_sum = lax.optimization_barrier(jnp.sum(kept_in.astype(jnp.float32), axis=0))
    summed = added([kept_sum, from_partner]).astype(jnp.bfloat16)
    return (summed, fresh_pages.reshape(2, 1, fresh_order.shape[0], PAGE, HEAD))


def solution(mesh):
    placed = (
        P(("req", "tp"), None),
        P(),
        P(None, "tp"),
        P("tp", None),
        P("req"),
        P("req"),
        P("req"),
        P("req"),
        P(None, "tp", "req", None, None),
    )
    return jax.shard_map(
        body,
        mesh=mesh,
        in_specs=placed,
        out_specs=(P(("req", "tp"), None), P(None, "tp", "req", None, None)),
        check_vma=False,
    )
```
